32 devices in a mesh: blocks: 2 (over y), tile: 16 (over z, x, core).
Axes of the slice: x: 2, y: 2, z: 4, core: 2. Of those that a mesh axis runs over, the one named last changes fastest.
Arguments:
- raw_views: bfloat16 [8, 1024, 32, 128], P(None, ('blocks', 'tile')), parts along dimension 1, as said below
- spread_taps: float32 [8, 2, 3, 31], replicated, may hold values from 0.0001 to 1, as said below
Outputs:
- estimate: float32 [1024, 32, 128], P(('blocks', 'tile')), parts along dimension 0
The draws below stay inside these ranges and needn't reach their ends.
There are 2 independent parts, one for each index of `blocks`. The reference program is written for one: setup_inputs(seed, part) draws one part's arguments, and reference() takes and returns one part's arrays. A program takes and returns all parts, laid end to end along the dimension named above; an argument that names none is the same for every part. Nothing has to cross between parts.
Inputs may be any that keep to these rules, and one draw needn't show every extreme that they name: `raw_views`: every entry is positive. `spread_taps`: every tap is positive.
All inputs are finite; a program needn't handle non-finite values.
Results may differ from the reference program's by a relative error of at most 0.0031.
Values may be sent and summed in bfloat16 or wider, within the bound.
No kernel may reach another device: no remote copies, remote signals or barrier semaphores. Data moves between devices by JAX's collectives and lax.ppermute only.
A program may use at most 64 MiB of HBM per device.

```python
import math
import jax
import jax.numpy as jnp
from jax import lax

VIEWS = 8
TAPS = 31
TERMS = 2
ITERS = 2
PLANES = 32
HEIGHT = 32
WIDTH = 128
RADIUS = 15
DEPTH = 512
N_TILE = 16


def draw_spread_taps(key, part):
    keys_all = jax.random.split(key, 2)
    offsets = jnp.arange(TAPS, dtype=jnp.float32) - RADIUS
    axis_widths = jnp.array([0.7, 0.35, 0.35], jnp.float32) * RADIUS
    broaden = 1.0 + 0.6 * jnp.arange(TERMS, dtype=jnp.float32)
    view_spread = jax.random.uniform(keys_all[0], (VIEWS, 1, 1), jnp.float32, 0.8, 1.25)
    spread_width = view_spread * axis_widths[None, None, :] * broaden[None, :, None]
    envelope = jnp.exp(-0.5 * (offsets / spread_width[..., None]) ** 2) / (spread_width[..., None] * 2.5066283)
    roughness = jax.random.uniform(keys_all[1], (VIEWS, TERMS, 3, TAPS), jnp.float32, 0.6, 1.4)
    term_weight = 0.35 ** jnp.arange(TERMS, dtype=jnp.float32)
    axis_first = (jnp.arange(3) == 0).astype(jnp.float32)
    weighting = axis_first[None, :] * term_weight[:, None] + (1.0 - axis_first[None, :])
    return jnp.clip(envelope * roughness * weighting[None, :, :, None], 0.0001, 1.0)


def draw_raw_views(key, part):
    keys_all = jax.random.split(key, 4)
    depth_pos = (jnp.arange(DEPTH, dtype=jnp.float32) + 0.5) / DEPTH
    alternate = jnp.arange(VIEWS, dtype=jnp.int32) % 2 * 2 - 1
    tilt_sign = jax.random.permutation(keys_all[0], alternate).astype(jnp.float32)
    gradient = math.log(3.0) + 0.5
    common_ramp = jnp.exp(gradient * depth_pos)
    tilt = jnp.exp(0.5 * tilt_sign[:, None] * (depth_pos[None, :] - 0.5) + 0.25)
    ramp = common_ramp[None, :] * tilt
    row_scale = jnp.exp(jax.random.uniform(keys_all[1], (DEPTH, HEIGHT), jnp.float32, math.log(0.3), math.log(3.0)))
    shared = jnp.exp(jax.random.uniform(keys_all[2], (DEPTH, HEIGHT, WIDTH), jnp.float32, -0.8, 0.8))
    own_part = jnp.exp(jax.random.uniform(keys_all[3], (VIEWS, DEPTH, HEIGHT, WIDTH), jnp.float32, -0.8, 0.8))
    mixture = 0.6 * shared[None] + 0.4 * own_part
    return (ramp[:, :, None, None] * row_scale[None, :, :, None] * mixture).astype(jnp.bfloat16)


def setup_inputs(seed: int = 0, part: int = 0) -> dict:
    seeds = jax.random.split(jax.random.key(seed), 3)
    part_keys = jax.random.split(jax.random.fold_in(seeds[2], part), 3)
    raw_views = draw_raw_views(jax.random.fold_in(jax.random.fold_in(seeds[2], part), 71), part)
    spread_taps = draw_spread_taps(jax.random.fold_in(seeds[2], 71), part)
    return {"raw_views": raw_views, "spread_taps": spread_taps}


def band_table(kernel_taps, length_in, length_out, tap_shift):
    tap_count = kernel_taps.shape[0]
    row_index = lax.broadcasted_iota(jnp.int32, (tap_count, length_in, length_out), 1)
    col_index = lax.broadcasted_iota(jnp.int32, (tap_count, length_in, length_out), 2)
    tap_index = lax.broadcasted_iota(jnp.int32, (tap_count, length_in, length_out), 0)
    selector = (row_index - col_index + tap_shift == tap_index).astype(jnp.float32)
    return jnp.einsum("k,kji->ji", kernel_taps.astype(jnp.float32), selector, precision=lax.Precision.HIGHEST)


def axis_depth(volume, kernel_taps):
    padded = jnp.pad(volume, ((RADIUS, RADIUS), (0, 0), (0, 0)))
    band_matrix = band_table(kernel_taps, PLANES + 2 * RADIUS, PLANES, 0)

    def one_block(start_plane):
        window_block = lax.dynamic_slice_in_dim(padded, start_plane, PLANES + 2 * RADIUS, 0)
        return jnp.einsum("jyx,ji->iyx", window_block.astype(jnp.float32), band_matrix)

    starts = jnp.arange(N_TILE, dtype=jnp.int32) * PLANES
    return lax.map(one_block, starts).reshape(DEPTH, HEIGHT, WIDTH)


def axis_height(volume, kernel_taps):
    band_matrix = band_table(kernel_taps, HEIGHT, HEIGHT, RADIUS)
    return jnp.einsum("zjx,ji->zix", volume.astype(jnp.float32), band_matrix)


def axis_width(volume, kernel_taps):
    band_matrix = band_table(kernel_taps, WIDTH, WIDTH, RADIUS)
    return jnp.einsum("zyj,ji->zyi", volume.astype(jnp.float32), band_matrix)


def blur(volume, kernel):
    summed = jnp.zeros(volume.shape, jnp.float32)
    for term_index in range(TERMS):
        first_pass = axis_depth(volume, kernel[term_index, 0]).astype(jnp.bfloat16)
        second = axis_height(first_pass, kernel[term_index, 1]).astype(jnp.bfloat16)
        summed = summed + axis_width(second, kernel[term_index, 2])
    return summed


def reference(raw_views, spread_taps):
    rounded_taps = spread_taps.astype(jnp.bfloat16)
    kernel = lax.optimization_barrier(rounded_taps).astype(jnp.float32)
    adjoint = kernel[:, :, :, ::-1]
    recorded = raw_views.astype(jnp.float32)
    totals = jnp.sum(recorded, axis=(1, 2, 3))
    scales = jnp.mean(totals) / totals
    scaled = recorded * scales[:, None, None, None]
    estimate = jnp.mean(scaled, axis=0)
    for iteration in range(ITERS):
        rounded = estimate.astype(jnp.bfloat16)
        factor = jnp.ones(estimate.shape, jnp.float32)
        for which_view in range(VIEWS):
            blurred = blur(rounded, kernel[which_view])
            quotient = (scaled[which_view] / blurred).astype(jnp.bfloat16)
            factor = factor * blur(quotient, adjoint[which_view])
        estimate = estimate * factor
    return estimate
```

```python
import functools

import jax
import jax.numpy as jnp
from jax import lax
from jax.experimental import pallas as pl
from jax.experimental.pallas import tpu as pltpu
from jax.sharding import PartitionSpec as P

ITERS = 2
LANES = 128
F32 = jnp.float32
BF16 = jnp.bfloat16


def toeplitz(row, rows, offset):
    lanes = row.shape[-1]
    wide = jnp.broadcast_to(row, (rows, lanes))
    return pltpu.roll(wide, (-offset) % lanes, 1, stride=1, stride_axis=0)


def depth_table(row, planes, halo, radius):
    return toeplitz(row, planes, radius - halo)


def width_table(row, width, radius):
    table = toeplitz(row, width, radius)
    r = lax.broadcasted_iota(jnp.int32, table.shape, 0)
    l = lax.broadcasted_iota(jnp.int32, table.shape, 1)
    return jnp.where(jnp.abs(l - r) <= radius, table, 0.0)


def height_table(rows, height, radius):
    lane = lax.broadcasted_iota(jnp.int32, (height, rows[0].shape[-1]), 1)
    table = jnp.zeros(lane.shape, F32)
    for t, row in enumerate(rows):
        part = toeplitz(row, height, radius - t * height)
        table = jnp.where(lane // height == t, part, table)
    return table[:, : len(rows) * height]


def store_width_table(bx_ref, rows, width, radius):
    for t, row in enumerate(rows):
        for s in range(len(rows)):
            block = (
                width_table(row, width, radius)
                if s == t
                else jnp.zeros((width, width), F32)
            )
            bx_ref[pl.ds(t * width, width), pl.ds(s * width, width)] = block.astype(BF16)


def column(parts, y):
    return jnp.concatenate([p[y] for p in parts], axis=0)


def width_pass(zs_at, bx, xs_ref, height, planes, terms, width, group):
    for g in range(height // group):
        lhs = jnp.concatenate(
            [
                jnp.concatenate([zs_at(y, t) for t in range(terms)], axis=1)
                for y in range(g * group, (g + 1) * group)
            ],
            axis=0,
        )
        out = jnp.dot(lhs, bx, preferred_element_type=F32)
        for t in range(terms):
            xs_ref[t, pl.ds(g * group * planes, group * planes), :] = out[
                :, t * width : (t + 1) * width
            ]


def height_pass(xs_ref, by, height, planes, terms, width, emit):
    for z in range(0, planes, 2):
        rhs = jnp.concatenate(
            [
                jnp.concatenate(
                    [
                        xs_ref[t, pl.ds(zz, height, stride=planes), :].astype(BF16)
                        for t in range(terms)
                    ],
                    axis=0,
                )
                for zz in (z, z + 1)
            ],
            axis=1,
        )
        out = jnp.dot(by, rhs, preferred_element_type=F32)
        emit(z, out[:, :width])
        emit(z + 1, out[:, width:])


def swap_out(qs_ref, lo_at, hi_at, height, planes):
    half = planes // 2
    for y in range(height):
        col = qs_ref[pl.ds(y, planes, stride=height), :].astype(BF16)
        lo_at(y, col[:half])
        hi_at(y, col[half:])


def first_body(scales_ref, raw_ref, est_ref, lo_ref, hi_ref):
    views, planes, height, width = raw_ref.shape
    for z in range(planes):
        acc = scales_ref[0] * raw_ref[0, z].astype(F32)
        for v in range(1, views):
            acc = acc + scales_ref[v] * raw_ref[v, z].astype(F32)
        est_ref[pl.ds(z * height, height), :] = acc / views

    def put(ref):
        def at(y, value):
            ref[y] = value
        return at

    swap_out(est_ref, put(lo_ref), put(hi_ref), height, planes)


def forward_body(radius, scales_ref, taps_ref, flip_ref, before, lo, hi, after, raw_ref,
                 qlo_ref, qhi_ref, bz_ref, bx_ref, zs_ref, xs_ref, qs_ref):
    views, planes, height, width = raw_ref.shape
    terms = taps_ref.shape[1]
    half = planes // 2
    for v in range(views):
        for t in range(terms):
            bz_ref[pl.ds((v * terms + t) * planes, planes), :] = depth_table(
                taps_ref[v, t, 0:1, :], planes, half, radius
            ).astype(BF16)[:, : 2 * planes]
    parts = (before, lo, hi, after)
    for y in range(0, height, 2):
        rhs = jnp.concatenate([column(parts, y), column(parts, y + 1)], axis=1)
        out = jnp.dot(bz_ref[...], rhs, preferred_element_type=F32).astype(BF16)
        zs_ref[y] = out[:, :width]
        zs_ref[y + 1] = out[:, width:]

    def view(v, carry):
        store_width_table(bx_ref, [flip_ref[v, t, 2:3, :] for t in range(terms)], width, radius)
        by = height_table([taps_ref[v, t, 1:2, :] for t in range(terms)], height, radius).astype(BF16)

        def zs_at(y, t):
            start = pl.multiple_of((v * terms + t) * planes, planes)
            return zs_ref[y, pl.ds(start, planes), :]

        width_pass(zs_at, bx_ref[...], xs_ref, height, planes, terms, width, 8)

        def emit(z, blurred):
            scaled = scales_ref[v] * raw_ref[v, z].astype(F32)
            qs_ref[pl.ds(z * height, height), :] = scaled / blurred

        height_pass(xs_ref, by, height, planes, terms, width, emit)

        def put(ref):
            def at(y, value):
                ref[v, y] = value
            return at

        swap_out(qs_ref, put(qlo_ref), put(qhi_ref), height, planes)
        return carry

    lax.fori_loop(0, views, view, 0)


def backward_body(radius, last, taps_ref, flip_ref, before, lo, hi, after, est_ref, *refs):
    if last:
        new_ref, bx_ref, zs_ref, xs_ref, fac_ref = refs
    else:
        new_ref, rlo_ref, rhi_ref, bx_ref, zs_ref, xs_ref, fac_ref = refs
    views, height, half, width = lo.shape
    planes = 2 * half
    terms = taps_ref.shape[1]
    fac_ref[...] = jnp.ones(fac_ref.shape, F32)

    def view(v, carry):
        bz = jnp.concatenate(
            [depth_table(flip_ref[v, t, 0:1, :], planes, half, radius) for t in range(terms)],
            axis=0,
        ).astype(BF16)[:, : 2 * planes]
        store_width_table(bx_ref, [taps_ref[v, t, 2:3, :] for t in range(terms)], width, radius)
        by = height_table([flip_ref[v, t, 1:2, :] for t in range(terms)], height, radius).astype(BF16)
        parts = [ref.at[v] for ref in (before, lo, hi, after)]
        for y in range(0, height, 2):
            rhs = jnp.concatenate([column(parts, y), column(parts, y + 1)], axis=1)
            out = jnp.dot(bz, rhs, preferred_element_type=F32).astype(BF16)
            zs_ref[y] = out[:, :width]
            zs_ref[y + 1] = out[:, width:]

        def zs_at(y, t):
            return zs_ref[y, t * planes : (t + 1) * planes, :]

        width_pass(zs_at, bx_ref[...], xs_ref, height, planes, terms, width, 8)

        def emit(z, blurred):
            rows = pl.ds(z * height, height)
            fac_ref[rows, :] = fac_ref[rows, :] * blurred

        height_pass(xs_ref, by, height, planes, terms, width, emit)
        return carry

    lax.fori_loop(0, views, view, 0)
    new_ref[...] = est_ref[...] * fac_ref[...]
    if not last:
        def put(ref):
            def at(y, value):
                ref[y] = value
            return at

        swap_out(new_ref, put(rlo_ref), put(rhi_ref), height, planes)


VMEM_SPEC = pl.BlockSpec(memory_space=pltpu.VMEM)
SMEM_SPEC = pl.BlockSpec(memory_space=pltpu.SMEM)


def local(raw_views, spread_taps):
    views, planes, height, width = raw_views.shape
    terms, tap_count = spread_taps.shape[1], spread_taps.shape[3]
    radius = (tap_count - 1) // 2
    half = planes // 2
    cells = planes * height
    size = lax.axis_size("tile")
    taps = spread_taps.astype(BF16).astype(F32)
    lane_pad = ((0, 0), (0, 0), (0, 0), (0, LANES - tap_count))
    flip = jnp.pad(taps[:, :, :, ::-1], lane_pad)
    taps = jnp.pad(taps, lane_pad)

    totals = lax.psum(jnp.sum(raw_views, axis=(1, 2, 3), dtype=F32), "tile")
    scales = jnp.mean(totals) / totals

    up = [(i, i + 1) for i in range(size - 1)]
    down = [(i + 1, i) for i in range(size - 1)]
    flat = jax.ShapeDtypeStruct((cells, width), F32)
    slab = jax.ShapeDtypeStruct((height, half, width), BF16)
    slabs = jax.ShapeDtypeStruct((views, height, half, width), BF16)
    params = pltpu.CompilerParams(vmem_limit_bytes=48 * 1024 * 1024)

    estimate, lo, hi = pl.pallas_call(
        first_body,
        out_shape=(flat, slab, slab),
        in_specs=[SMEM_SPEC, VMEM_SPEC],
        out_specs=(VMEM_SPEC,) * 3,
        compiler_params=params,
        name="first",
    )(scales, raw_views)

    forward = pl.pallas_call(
        functools.partial(forward_body, radius),
        out_shape=(slabs, slabs),
        in_specs=[SMEM_SPEC] + [VMEM_SPEC] * 7,
        out_specs=(VMEM_SPEC,) * 2,
        scratch_shapes=[
            pltpu.VMEM((views * terms * planes, 2 * planes), BF16),
            pltpu.VMEM((terms * width, terms * width), BF16),
            pltpu.VMEM((height, views * terms * planes, width), BF16),
            pltpu.VMEM((terms, cells, width), F32),
            pltpu.VMEM((cells, width), F32),
        ],
        compiler_params=params,
        name="forward",
    )

    def backward(last):
        return pl.pallas_call(
            functools.partial(backward_body, radius, last),
            out_shape=(flat,) if last else (flat, slab, slab),
            in_specs=[VMEM_SPEC] * 7,
            out_specs=(VMEM_SPEC,) * (1 if last else 3),
            scratch_shapes=[
                pltpu.VMEM((terms * width, terms * width), BF16),
                pltpu.VMEM((height, terms * planes, width), BF16),
                pltpu.VMEM((terms, cells, width), F32),
                pltpu.VMEM((cells, width), F32),
            ],
            compiler_params=params,
            name="backward",
        )

    for iteration in range(ITERS):
        last = iteration == ITERS - 1
        before = lax.ppermute(hi, "tile", up)
        after = lax.ppermute(lo, "tile", down)
        qlo, qhi = forward(scales, taps, flip, before, lo, hi, after, raw_views)
        qbefore = lax.ppermute(qhi, "tile", up)
        qafter = lax.ppermute(qlo, "tile", down)
        out = backward(last)(taps, flip, qbefore, qlo, qhi, qafter, estimate)
        if last:
            (estimate,) = out
        else:
            estimate, lo, hi = out
    return estimate.reshape(planes, height, width)


def solution(mesh):
    return jax.shard_map(
        local,
        mesh=mesh,
        in_specs=(P(None, ("blocks", "tile"), None, None), P()),
        out_specs=P(("blocks", "tile"), None, None),
        check_vma=False,
    )
```

```python
import functools

import jax
import jax.numpy as jnp
from jax import lax
from jax.experimental import pallas as pl
from jax.experimental.pallas import tpu as pltpu
from jax.sharding import PartitionSpec as P

ITERS = 2
LANES = 128
F32 = jnp.float32
BF16 = jnp.bfloat16


def toeplitz(row, rows, offset):
    lanes = row.shape[-1]
    wide = jnp.broadcast_to(row, (rows, lanes))
    return pltpu.roll(wide, (-offset) % lanes, 1, stride=1, stride_axis=0)


def depth_table(row, planes, halo, radius):
    return toeplitz(row, planes, radius - halo)


def width_table(row, width, radius):
    table = toeplitz(row, width, radius)
    r = lax.broadcasted_iota(jnp.int32, table.shape, 0)
    l = lax.broadcasted_iota(jnp.int32, table.shape, 1)
    return jnp.where(jnp.abs(l - r) <= radius, table, 0.0)


def height_table(rows, height, radius):
    lane = lax.broadcasted_iota(jnp.int32, (height, rows[0].shape[-1]), 1)
    table = jnp.zeros(lane.shape, F32)
    for t, row in enumerate(rows):
        part = toeplitz(row, height, radius - t * height)
        table = jnp.where(lane // height == t, part, table)
    return table[:, : len(rows) * height]


def store_width_table(bx_ref, rows, width, radius):
    for t, row in enumerate(rows):
        for s in range(len(rows)):
            block = (
                width_table(row, width, radius)
                if s == t
                else jnp.zeros((width, width), F32)
            )
            bx_ref[pl.ds(t * width, width), pl.ds(s * width, width)] = block.astype(BF16)


def column(parts, y):
    return jnp.concatenate([p[y] for p in parts], axis=0)


def width_pass(zs_at, bx, xs_ref, height, planes, terms, width, group):
    for g in range(height // group):
        lhs = jnp.concatenate(
            [
                jnp.concatenate([zs_at(y, t) for t in range(terms)], axis=1)
                for y in range(g * group, (g + 1) * group)
            ],
            axis=0,
        )
        out = jnp.dot(lhs, bx, preferred_element_type=F32)
        for t in range(terms):
            for i in range(group):
                xs_ref[t, pl.ds((g * group + i) * (planes + 1), planes), :] = out[
                    i * planes : (i + 1) * planes, t * width : (t + 1) * width
                ]


def height_pass(xs_ref, by, height, planes, terms, width, emit):
    for z in range(0, planes, 2):
        rhs = jnp.concatenate(
            [
                jnp.concatenate(
                    [
                        xs_ref[t, pl.ds(zz, height, stride=planes + 1), :].astype(BF16)
                        for t in range(terms)
                    ],
                    axis=0,
                )
                for zz in (z, z + 1)
            ],
            axis=1,
        )
        out = jnp.dot(by, rhs, preferred_element_type=F32)
        emit(z, out[:, :width])
        emit(z + 1, out[:, width:])


def swap_out(qs_ref, lo_at, hi_at, height, planes):
    half = planes // 2
    for y in range(height):
        col = qs_ref[pl.ds(y, planes, stride=height + 1), :].astype(BF16)
        lo_at(y, col[:half])
        hi_at(y, col[half:])


def first_body(scales_ref, raw_ref, est_ref, lo_ref, hi_ref, qs_ref):
    views, planes, height, width = raw_ref.shape
    for z in range(planes):
        acc = scales_ref[0] * raw_ref[0, z].astype(F32)
        for v in range(1, views):
            acc = acc + scales_ref[v] * raw_ref[v, z].astype(F32)
        acc = acc / views
        est_ref[pl.ds(z * height, height), :] = acc
        qs_ref[pl.ds(z * (height + 1), height), :] = acc

    def put(ref):
        def at(y, value):
            ref[y] = value
        return at

    swap_out(qs_ref, put(lo_ref), put(hi_ref), height, planes)


def forward_body(radius, scales_ref, taps_ref, flip_ref, before, lo, hi, after, raw_ref,
                 qlo_ref, qhi_ref, bz_ref, bx_ref, zs_ref, xs_ref, qs_ref):
    views, planes, height, width = raw_ref.shape
    terms = taps_ref.shape[1]
    half = planes // 2
    for v in range(views):
        for t in range(terms):
            bz_ref[pl.ds((v * terms + t) * planes, planes), :] = depth_table(
                taps_ref[v, t, 0:1, :], planes, half, radius
            ).astype(BF16)[:, : 2 * planes]
    parts = (before, lo, hi, after)
    for y in range(0, height, 2):
        rhs = jnp.concatenate([column(parts, y), column(parts, y + 1)], axis=1)
        out = jnp.dot(bz_ref[...], rhs, preferred_element_type=F32).astype(BF16)
        zs_ref[y] = out[:, :width]
        zs_ref[y + 1] = out[:, width:]

    def view(v, carry):
        store_width_table(bx_ref, [flip_ref[v, t, 2:3, :] for t in range(terms)], width, radius)
        by = height_table([taps_ref[v, t, 1:2, :] for t in range(terms)], height, radius).astype(BF16)

        def zs_at(y, t):
            start = pl.multiple_of((v * terms + t) * planes, planes)
            return zs_ref[y, pl.ds(start, planes), :]

        width_pass(zs_at, bx_ref[...], xs_ref, height, planes, terms, width, 8)

        def emit(z, blurred):
            scaled = scales_ref[v] * raw_ref[v, z].astype(F32)
            qs_ref[pl.ds(z * (height + 1), height), :] = scaled / blurred

        height_pass(xs_ref, by, height, planes, terms, width, emit)

        def put(ref):
            def at(y, value):
                ref[v, y] = value
            return at

        swap_out(qs_ref, put(qlo_ref), put(qhi_ref), height, planes)
        return carry

    lax.fori_loop(0, views, view, 0)


def backward_body(radius, last, taps_ref, flip_ref, before, lo, hi, after, est_ref, *refs):
    if last:
        new_ref, bx_ref, zs_ref, xs_ref, fac_ref, qs_ref = refs
    else:
        new_ref, rlo_ref, rhi_ref, bx_ref, zs_ref, xs_ref, fac_ref, qs_ref = refs
    views, height, half, width = lo.shape
    planes = 2 * half
    terms = taps_ref.shape[1]
    fac_ref[...] = jnp.ones(fac_ref.shape, F32)

    def view(v, carry):
        bz = jnp.concatenate(
            [depth_table(flip_ref[v, t, 0:1, :], planes, half, radius) for t in range(terms)],
            axis=0,
        ).astype(BF16)[:, : 2 * planes]
        store_width_table(bx_ref, [taps_ref[v, t, 2:3, :] for t in range(terms)], width, radius)
        by = height_table([flip_ref[v, t, 1:2, :] for t in range(terms)], height, radius).astype(BF16)
        parts = [ref.at[v] for ref in (before, lo, hi, after)]
        for y in range(0, height, 2):
            rhs = jnp.concatenate([column(parts, y), column(parts, y + 1)], axis=1)
            out = jnp.dot(bz, rhs, preferred_element_type=F32).astype(BF16)
            zs_ref[y] = out[:, :width]
            zs_ref[y + 1] = out[:, width:]

        def zs_at(y, t):
            return zs_ref[y, t * planes : (t + 1) * planes, :]

        width_pass(zs_at, bx_ref[...], xs_ref, height, planes, terms, width, 8)

        def emit(z, blurred):
            rows = pl.ds(z * height, height)
            fac_ref[rows, :] = fac_ref[rows, :] * blurred

        height_pass(xs_ref, by, height, planes, terms, width, emit)
        return carry

    lax.fori_loop(0, views, view, 0)
    for z in range(planes):
        rows = pl.ds(z * height, height)
        new = est_ref[rows, :] * fac_ref[rows, :]
        new_ref[rows, :] = new
        if not last:
            qs_ref[pl.ds(z * (height + 1), height), :] = new
    if not last:
        def put(ref):
            def at(y, value):
                ref[y] = value
            return at

        swap_out(qs_ref, put(rlo_ref), put(rhi_ref), height, planes)


VMEM_SPEC = pl.BlockSpec(memory_space=pltpu.VMEM)
SMEM_SPEC = pl.BlockSpec(memory_space=pltpu.SMEM)


def local(raw_views, spread_taps):
    views, planes, height, width = raw_views.shape
    terms, tap_count = spread_taps.shape[1], spread_taps.shape[3]
    radius = (tap_count - 1) // 2
    half = planes // 2
    cells = planes * height
    size = lax.axis_size("tile")
    taps = spread_taps.astype(BF16).astype(F32)
    lane_pad = ((0, 0), (0, 0), (0, 0), (0, LANES - tap_count))
    flip = jnp.pad(taps[:, :, :, ::-1], lane_pad)
    taps = jnp.pad(taps, lane_pad)

    totals = lax.psum(jnp.sum(raw_views, axis=(1, 2, 3), dtype=F32), "tile")
    scales = jnp.mean(totals) / totals

    up = [(i, i + 1) for i in range(size - 1)]
    down = [(i + 1, i) for i in range(size - 1)]
    flat = jax.ShapeDtypeStruct((cells, width), F32)
    slab = jax.ShapeDtypeStruct((height, half, width), BF16)
    slabs = jax.ShapeDtypeStruct((views, height, half, width), BF16)
    params = pltpu.CompilerParams(vmem_limit_bytes=48 * 1024 * 1024)

    estimate, lo, hi = pl.pallas_call(
        first_body,
        out_shape=(flat, slab, slab),
        in_specs=[SMEM_SPEC, VMEM_SPEC],
        out_specs=(VMEM_SPEC,) * 3,
        scratch_shapes=[pltpu.VMEM((planes * (height + 1), width), F32)],
        compiler_params=params,
        name="first",
    )(scales, raw_views)

    forward = pl.pallas_call(
        functools.partial(forward_body, radius),
        out_shape=(slabs, slabs),
        in_specs=[SMEM_SPEC] + [VMEM_SPEC] * 7,
        out_specs=(VMEM_SPEC,) * 2,
        scratch_shapes=[
            pltpu.VMEM((views * terms * planes, 2 * planes), BF16),
            pltpu.VMEM((terms * width, terms * width), BF16),
            pltpu.VMEM((height, views * terms * planes, width), BF16),
            pltpu.VMEM((terms, height * (planes + 1), width), F32),
            pltpu.VMEM((planes * (height + 1), width), F32),
        ],
        compiler_params=params,
        name="forward",
    )

    def backward(last):
        return pl.pallas_call(
            functools.partial(backward_body, radius, last),
            out_shape=(flat,) if last else (flat, slab, slab),
            in_specs=[VMEM_SPEC] * 7,
            out_specs=(VMEM_SPEC,) * (1 if last else 3),
            scratch_shapes=[
                pltpu.VMEM((terms * width, terms * width), BF16),
                pltpu.VMEM((height, terms * planes, width), BF16),
                pltpu.VMEM((terms, height * (planes + 1), width), F32),
                pltpu.VMEM((cells, width), F32),
                pltpu.VMEM((planes * (height + 1), width), F32),
            ],
            compiler_params=params,
            name="backward",
        )

    for iteration in range(ITERS):
        last = iteration == ITERS - 1
        before = lax.ppermute(hi, "tile", up)
        after = lax.ppermute(lo, "tile", down)
        qlo, qhi = forward(scales, taps, flip, before, lo, hi, after, raw_views)
        qbefore = lax.ppermute(qhi, "tile", up)
        qafter = lax.ppermute(qlo, "tile", down)
        out = backward(last)(taps, flip, qbefore, qlo, qhi, qafter, estimate)
        if last:
            (estimate,) = out
        else:
            estimate, lo, hi = out
    return estimate.reshape(planes, height, width)


def solution(mesh):
    return jax.shard_map(
        local,
        mesh=mesh,
        in_specs=(P(None, ("blocks", "tile"), None, None), P()),
        out_specs=P(("blocks", "tile"), None, None),
        check_vma=False,
    )
```

```python
import functools

import jax
import jax.numpy as jnp
from jax import lax
from jax.experimental import pallas as pl
from jax.experimental.pallas import tpu as pltpu
from jax.sharding import PartitionSpec as P

ITERS = 2
LANES = 128
F32 = jnp.float32
BF16 = jnp.bfloat16


def toeplitz(row, rows, offset):
    lanes = row.shape[-1]
    wide = jnp.broadcast_to(row, (rows, lanes))
    return pltpu.roll(wide, (-offset) % lanes, 1, stride=1, stride_axis=0)


def depth_table(row, planes, radius, swapped):
    offset = radius - planes // 2
    lanes = row.shape[-1]
    ahead = pltpu.roll(row, lanes - planes, 1)
    behind = pltpu.roll(row, planes, 1)
    near = toeplitz(jnp.where(swapped == 1, ahead, row), planes, offset)
    far = toeplitz(jnp.where(swapped == 1, behind, row), planes, offset)
    lane = lax.broadcasted_iota(jnp.int32, near.shape, 1)
    return jnp.where(lane < planes, near, far).astype(BF16)[:, : 2 * planes]


def width_table(row, width, radius):
    table = toeplitz(row, width, radius)
    r = lax.broadcasted_iota(jnp.int32, table.shape, 0)
    l = lax.broadcasted_iota(jnp.int32, table.shape, 1)
    return jnp.where(jnp.abs(l - r) <= radius, table, 0.0)


def height_table(rows, height, radius):
    lane = lax.broadcasted_iota(jnp.int32, (height, rows[0].shape[-1]), 1)
    table = jnp.zeros(lane.shape, F32)
    for t, row in enumerate(rows):
        part = toeplitz(row, height, radius - t * height)
        table = jnp.where(lane // height == t, part, table)
    return table[:, : len(rows) * height].astype(BF16)


def store_width_table(bx_ref, rows, width, radius):
    for t, row in enumerate(rows):
        for s in range(len(rows)):
            block = (
                width_table(row, width, radius)
                if s == t
                else jnp.zeros((width, width), F32)
            )
            bx_ref[pl.ds(t * width, width), pl.ds(s * width, width)] = block.astype(BF16)


def depth_pass(parts, bz, zs_ref):
    height, _, width = parts[0].shape
    for y in range(0, height, 2):
        rhs = jnp.concatenate(
            [jnp.concatenate([p[yy] for p in parts], axis=0) for yy in (y, y + 1)], axis=1
        )
        out = jnp.dot(bz, rhs, preferred_element_type=F32).astype(BF16)
        zs_ref[y] = out[:, :width]
        zs_ref[y + 1] = out[:, width:]


def width_pass(zs_at, bx, xs_ref, height, planes, terms, width, group):
    for g in range(0, height, group):
        lhs = jnp.concatenate(
            [
                jnp.concatenate([zs_at(y, t) for t in range(terms)], axis=1)
                for y in range(g, g + group)
            ],
            axis=0,
        )
        out = jnp.dot(lhs, bx, preferred_element_type=F32)
        for t in range(terms):
            for i in range(group):
                xs_ref[t, pl.ds((g + i) * (planes + 1), planes), :] = out[
                    i * planes : (i + 1) * planes, t * width : (t + 1) * width
                ]


def height_pair(xs_ref, by, z, height, planes, terms, width):
    rhs = jnp.concatenate(
        [
            jnp.concatenate(
                [
                    xs_ref[t, pl.ds(zz, height, stride=planes + 1), :].astype(BF16)
                    for t in range(terms)
                ],
                axis=0,
            )
            for zz in (z, z + 1)
        ],
        axis=1,
    )
    out = jnp.dot(by, rhs, preferred_element_type=F32)
    return out[:, :width], out[:, width:]


def swap_out(qs_ref, put, height, planes):
    for y in range(height):
        put(y, qs_ref[pl.ds(y, planes, stride=height + 1), :].astype(BF16))


def sums_body(even_ref, raw_ref, sums_ref, near_ref, far_ref):
    views, planes, height, width = raw_ref.shape
    half = planes // 2
    even = even_ref[0]
    for v in range(views):
        acc = jnp.zeros((height, width), F32)
        for z in range(planes):
            acc = acc + raw_ref[v, z].astype(F32)
        row = jnp.sum(acc, axis=0, keepdims=True)
        sums_ref[pl.ds(v, 1), :] = jnp.broadcast_to(
            jnp.sum(row, axis=1, keepdims=True), (1, width)
        )
        near_ref[v] = raw_ref[v, pl.ds(even * half, half)]
        far_ref[v] = raw_ref[v, pl.ds((1 - even) * half, half)]


def scale_rows(totals_ref):
    totals = totals_ref[...]
    return jnp.mean(totals, axis=0, keepdims=True) / totals


def first_body(totals_ref, raw_ref, est_ref, slab_ref, qs_ref):
    views, planes, height, width = raw_ref.shape
    scales = scale_rows(totals_ref)
    for z in range(planes):
        acc = scales[0:1] * raw_ref[0, z].astype(F32)
        for v in range(1, views):
            acc = acc + scales[v : v + 1] * raw_ref[v, z].astype(F32)
        acc = acc / views
        est_ref[pl.ds(z * height, height), :] = acc
        qs_ref[pl.ds(z * (height + 1), height), :] = acc

    def put(y, value):
        slab_ref[y] = value

    swap_out(qs_ref, put, height, planes)


def forward_body(radius, swapped_ref, pad_ref, totals_ref, taps_ref, flip_ref, own_ref, part_ref,
                 raw_ref, raw_part_ref, q_ref, bz_ref, bx_ref, zs_ref, xs_ref, qs_ref, sc_ref):
    views, planes, height, width = raw_ref.shape
    terms = taps_ref.shape[1]
    half = planes // 2
    swapped = swapped_ref[0]
    pad = pad_ref[0]
    sc_ref[...] = scale_rows(totals_ref)
    for v in range(views):
        for t in range(terms):
            bz_ref[pl.ds((v * terms + t) * planes, planes), :] = depth_table(
                taps_ref[v, t, 0:1, :], planes, radius, swapped
            )
    depth_pass((own_ref, part_ref), bz_ref[...], zs_ref)

    def view(v, carry):
        store_width_table(bx_ref, [flip_ref[v, t, 2:3, :] for t in range(terms)], width, radius)
        by = height_table([taps_ref[v, t, 1:2, :] for t in range(terms)], height, radius)
        scale = sc_ref[pl.ds(v, 1), :]

        def zs_at(y, t):
            start = pl.multiple_of((v * terms + t) * planes, planes)
            return zs_ref[y, pl.ds(start, planes), :]

        width_pass(zs_at, bx_ref[...], xs_ref, height, planes, terms, width, 8)
        for partner in (False, True):
            base = (1 - swapped if partner else swapped) * half
            for r in range(0, half, 2):
                pair = height_pair(xs_ref, by, base + r, height, planes, terms, width)
                for i, blurred in enumerate(pair):
                    if partner:
                        raw = raw_part_ref[v, r + i]
                        blurred = blurred + pad
                    else:
                        raw = raw_ref[v, (1 - swapped) * half + r + i]
                    rows = pl.ds((base + r + i) * (height + 1), height)
                    qs_ref[rows, :] = scale * raw.astype(F32) / blurred

        def put(y, value):
            q_ref[v, y] = value

        swap_out(qs_ref, put, height, planes)
        return carry

    lax.fori_loop(0, views, view, 0)


def backward_body(radius, last, swapped_ref, taps_ref, flip_ref, near_ref, far_ref, est_ref, *refs):
    if last:
        new_ref, bx_ref, zs_ref, xs_ref, fac_ref, qs_ref = refs
    else:
        new_ref, slab_ref, bx_ref, zs_ref, xs_ref, fac_ref, qs_ref = refs
    views, height, planes, width = near_ref.shape
    terms = taps_ref.shape[1]
    swapped = swapped_ref[0]
    fac_ref[...] = jnp.ones(fac_ref.shape, F32)

    def view(v, carry):
        bz = jnp.concatenate(
            [depth_table(flip_ref[v, t, 0:1, :], planes, radius, swapped) for t in range(terms)],
            axis=0,
        )
        store_width_table(bx_ref, [taps_ref[v, t, 2:3, :] for t in range(terms)], width, radius)
        by = height_table([flip_ref[v, t, 1:2, :] for t in range(terms)], height, radius)
        depth_pass((near_ref.at[v], far_ref.at[v]), bz, zs_ref)

        def zs_at(y, t):
            return zs_ref[y, t * planes : (t + 1) * planes, :]

        width_pass(zs_at, bx_ref[...], xs_ref, height, planes, terms, width, 8)
        for z in range(0, planes, 2):
            pair = height_pair(xs_ref, by, z, height, planes, terms, width)
            for i, blurred in enumerate(pair):
                rows = pl.ds((z + i) * height, height)
                fac_ref[rows, :] = fac_ref[rows, :] * blurred
        return carry

    lax.fori_loop(0, views, view, 0)
    for z in range(planes):
        rows = pl.ds(z * height, height)
        new = est_ref[rows, :] * fac_ref[rows, :]
        new_ref[rows, :] = new
        if not last:
            qs_ref[pl.ds(z * (height + 1), height), :] = new
    if not last:

        def put(y, value):
            slab_ref[y] = value

        swap_out(qs_ref, put, height, planes)


VMEM_SPEC = pl.BlockSpec(memory_space=pltpu.VMEM)
SMEM_SPEC = pl.BlockSpec(memory_space=pltpu.SMEM)


def sum_over(value, axis, size):
    if size & (size - 1):
        return lax.psum(value, axis)
    step = 1
    while step < size:
        value = value + lax.ppermute(value, axis, [(i, i ^ step) for i in range(size)])
        step *= 2
    return value


def local(raw_views, spread_taps):
    views, planes, height, width = raw_views.shape
    terms, tap_count = spread_taps.shape[1], spread_taps.shape[3]
    radius = (tap_count - 1) // 2
    half = planes // 2
    cells = planes * height
    size = lax.axis_size("tile")
    place = lax.axis_index("tile")
    odd = lax.rem(place, 2)
    even = 1 - odd
    near_pairs = [(i, i + 1) for i in range(0, size - 1, 2)]
    far_pairs = [(i, i + 1) for i in range(1, size - 1, 2)]
    near_pairs += [(j, i) for i, j in near_pairs]
    far_pairs += [(j, i) for i, j in far_pairs]
    near_at = place + even - odd
    far_at = place + odd - even

    def missing(at):
        return jnp.where((at < 0) | (at >= size), 1.0, 0.0).astype(F32).reshape(1)

    near_pad, far_pad = missing(near_at), missing(far_at)
    even, odd = even.reshape(1), odd.reshape(1)

    taps = spread_taps.astype(BF16).astype(F32)
    lane_pad = ((0, 0), (0, 0), (0, 0), (0, LANES - tap_count))
    flip = jnp.pad(taps[:, :, :, ::-1], lane_pad)
    taps = jnp.pad(taps, lane_pad)

    flat = jax.ShapeDtypeStruct((cells, width), F32)
    slab = jax.ShapeDtypeStruct((height, planes, width), BF16)
    halves = jax.ShapeDtypeStruct((views, half, height, width), BF16)
    windows = jax.ShapeDtypeStruct((views, height, planes, width), BF16)
    params = pltpu.CompilerParams(vmem_limit_bytes=24 * 1024 * 1024)
    turned = pltpu.VMEM((planes * (height + 1), width), F32)
    spread = pltpu.VMEM((terms, height * (planes + 1), width), F32)
    square = pltpu.VMEM((terms * width, terms * width), BF16)

    sums, raw_near, raw_far = pl.pallas_call(
        sums_body,
        out_shape=(jax.ShapeDtypeStruct((views, width), F32), halves, halves),
        in_specs=[SMEM_SPEC, VMEM_SPEC],
        out_specs=(VMEM_SPEC,) * 3,
        compiler_params=params,
        name="sums",
    )(even, raw_views)
    raw_far = lax.ppermute(raw_far, "tile", far_pairs)
    raw_near = lax.ppermute(raw_near, "tile", near_pairs)
    totals = sum_over(sums, "tile", size)

    estimate, own = pl.pallas_call(
        first_body,
        out_shape=(flat, slab),
        in_specs=[VMEM_SPEC, VMEM_SPEC],
        out_specs=(VMEM_SPEC,) * 2,
        scratch_shapes=[turned],
        compiler_params=params,
        name="first",
    )(totals, raw_views)

    forward = pl.pallas_call(
        functools.partial(forward_body, radius),
        out_shape=windows,
        in_specs=[SMEM_SPEC] * 2 + [VMEM_SPEC] * 7,
        out_specs=VMEM_SPEC,
        scratch_shapes=[
            pltpu.VMEM((views * terms * planes, 2 * planes), BF16),
            square,
            pltpu.VMEM((height, views * terms * planes, width), BF16),
            spread,
            turned,
            pltpu.VMEM((views, width), F32),
        ],
        compiler_params=params,
        name="forward",
    )

    def backward(last):
        return pl.pallas_call(
            functools.partial(backward_body, radius, last),
            out_shape=(flat,) if last else (flat, slab),
            in_specs=[SMEM_SPEC] + [VMEM_SPEC] * 5,
            out_specs=(VMEM_SPEC,) * (1 if last else 2),
            scratch_shapes=[
                square,
                pltpu.VMEM((height, terms * planes, width), BF16),
                spread,
                pltpu.VMEM((cells, width), F32),
                turned,
            ],
            compiler_params=params,
            name="backward",
        )

    for iteration in range(ITERS):
        last = iteration == ITERS - 1
        far = lax.ppermute(own, "tile", far_pairs)
        near = lax.ppermute(own, "tile", near_pairs)
        q_near = forward(odd, near_pad, totals, taps, flip, own, near, raw_views, raw_near)
        q_far = forward(even, far_pad, totals, taps, flip, own, far, raw_views, raw_far)
        out = backward(last)(even, taps, flip, q_near, q_far, estimate)
        if last:
            (estimate,) = out
        else:
            estimate, own = out
    return estimate.reshape(planes, height, width)


def solution(mesh):
    return jax.shard_map(
        local,
        mesh=mesh,
        in_specs=(P(None, ("blocks", "tile"), None, None), P()),
        out_specs=P(("blocks", "tile"), None, None),
        check_vma=False,
    )
```
